128 devices in a mesh: gx: 8 (over z, core), gy: 16 (over x, y).
Axes of the slice: x: 4, y: 4, z: 4, core: 2. Of those that a mesh axis runs over, the one named last changes fastest.
Arguments:
- leaf_front: float32 [12288, 24576], P('gx', 'gy'), may hold values from -18 to 18, as said below
- place_pairs: int32 [8, 128], P('gx', 'gy'), may hold values from 0 to 11, as said below
- place_quads: int32 [8, 128], P('gx', 'gy'), may hold values from 0 to 11, as said below
Outputs:
- pair_panel: float32 [12288, 8192], P('gx', 'gy')
- quad_panel: float32 [12288, 8192], P('gx', 'gy')
- quad_update: float32 [8192, 16384], P('gx', 'gy')
The draws below stay inside these ranges and needn't reach their ends.
Inputs may be any that keep to these rules, and one draw needn't show every extreme that they name: `leaf_front`: each tile is symmetric positive definite. `place_pairs`: each device's 8 entries are distinct; the two devices (q, j) and (q + 4, j) both name blocks 0 to 3, and each names 4 of the other blocks that the other does not name. `place_quads`: devices (q, j) and (q + 4, j) hold equal rows; each row's 8 entries are distinct; the rows of (q, r) and (q, r + 8) both name blocks 0 to 3, and each names 4 of the other blocks that the other does not name.
All inputs are finite; a program needn't handle non-finite values.
Results may differ from the reference program's by a relative error of at most 0.0003.
Values sent between devices are 32-bit elements; how exact they have to be, the bound alone decides.
A program may use at most 192 MiB of HBM per device.

```python
import jax
import jax.numpy as jnp
from jax import lax

BLK = 128
KB = 8
NI = 512
KS = 4
NB = 1024
NS = 512
NJ = 1536
NL = 1536
N_GX = 8
N_GY = 16


def draw_leaf_front(key, part):
    devices_total = N_GX * N_GY
    subkeys = jax.random.split(jax.random.fold_in(key, 3), devices_total)
    gen_rank = max(NL // 4, 8)

    def one_device(device_key):
        key_gen, key_diag = jax.random.split(device_key, 2)
        generator = jnp.clip(jax.random.normal(key_gen, (NL, gen_rank), jnp.float32), -4.0, 4.0)
        diag_shift = jnp.exp(jax.random.uniform(key_diag, (NL,), jnp.float32, -0.6931, 0.4055))
        gram_matrix = jnp.dot(generator, generator.T, precision=lax.Precision.HIGHEST) / gen_rank
        gram_matrix = 0.5 * (gram_matrix + gram_matrix.T)
        matrix = gram_matrix + jnp.diag(diag_shift)
        return matrix
    matrices = jax.vmap(one_device)(subkeys)
    return matrices.reshape(N_GX, N_GY, NL, NL).transpose(0, 2, 1, 3).reshape(N_GX * NL, N_GY * NL)


def placement_rows(key, parity):
    subkeys = jax.random.split(key, parity.shape[0])

    def one_row(row_key, side):
        targets = jnp.concatenate([jnp.arange(KS, dtype=jnp.int32), (KS + side * (KB - KS) + jnp.arange(KB - KS)).astype(jnp.int32)])
        return jax.random.permutation(row_key, targets)
    return jax.vmap(one_row)(subkeys, parity)


def draw_place_pairs(key, part):
    devices_total = N_GX * N_GY
    parity = (jnp.arange(devices_total) // N_GY >= N_GX // 2).astype(jnp.int32)
    indices = placement_rows(jax.random.fold_in(key, 11), parity)
    return indices.reshape(N_GX, N_GY * KB)


def draw_place_quads(key, part):
    groups_total = N_GX // 2 * N_GY
    parity = (jnp.arange(groups_total) % N_GY >= N_GY // 2).astype(jnp.int32)
    indices = placement_rows(jax.random.fold_in(key, 23), parity).reshape(N_GX // 2, N_GY, KB)
    return jnp.concatenate([indices, indices], axis=0).reshape(N_GX, N_GY * KB)


def setup_inputs(seed: int = 0) -> dict:
    seeds = jax.random.split(jax.random.key(seed), 4)
    return {
        "leaf_front": draw_leaf_front(jax.random.fold_in(seeds[3], 71), 0),
        "place_pairs": draw_place_pairs(jax.random.fold_in(seeds[3], 71), 0),
        "place_quads": draw_place_quads(jax.random.fold_in(seeds[3], 71), 0),
    }


def leaf_update(front_tile):
    interior = jnp.linalg.cholesky(front_tile[:NI, :NI])
    coupled = jax.scipy.linalg.solve_triangular(interior, front_tile[:NI, NI:], lower=True)
    return front_tile[NI:, NI:] - jnp.dot(coupled.T, coupled, precision=lax.Precision.HIGHEST)

def extend_add(update, placement):
    indices = (placement[:, None] * BLK + jnp.arange(BLK)[None, :]).reshape(-1).astype(jnp.int32)
    return jnp.zeros((NJ, NJ), update.dtype).at[indices[:, None], indices[None, :]].add(update)

def partial_factor(joined):
    corner = jnp.linalg.cholesky(joined[:NS, :NS])
    coupled = jax.scipy.linalg.solve_triangular(corner, joined[:NS, NS:], lower=True)
    factor_panel = jnp.concatenate([corner, coupled.T], axis=0)
    update = joined[NS:, NS:] - jnp.dot(coupled.T, coupled, precision=lax.Precision.HIGHEST)
    return (factor_panel, update)

def merge_children(operands):
    first_update, first_place, second_update, second_place = operands
    joined = extend_add(first_update, first_place) + extend_add(second_update, second_place)
    return partial_factor(joined)

def tiles_out(stacked, rows_rep, cols_rep):
    spread = jnp.tile(stacked, (rows_rep, cols_rep, 1, 1))
    return spread.transpose(0, 2, 1, 3).reshape(spread.shape[0] * spread.shape[2], spread.shape[1] * spread.shape[3])

def reference(leaf_front, place_pairs, place_quads):
    all_fronts = leaf_front.reshape(N_GX, NL, N_GY, NL).transpose(0, 2, 1, 3).reshape(N_GX * N_GY, NL, NL)
    leaf_updates = lax.map(leaf_update, all_fronts).reshape(N_GX, N_GY, NB, NB)
    pair_places = place_pairs.reshape(N_GX, N_GY, KB)
    quad_places = place_quads.reshape(N_GX, N_GY, KB)
    half_gx = N_GX // 2
    half_gy = N_GY // 2
    level_one = (leaf_updates[:half_gx].reshape(-1, NB, NB), pair_places[:half_gx].reshape(-1, KB), leaf_updates[half_gx:].reshape(-1, NB, NB), pair_places[half_gx:].reshape(-1, KB))
    panels_one, updates_one = lax.map(merge_children, level_one)
    panels_one = panels_one.reshape(half_gx, N_GY, NJ, NS)
    updates_one = updates_one.reshape(half_gx, N_GY, NB, NB)
    level_two = (updates_one[:, :half_gy].reshape(-1, NB, NB), quad_places[:half_gx, :half_gy].reshape(-1, KB), updates_one[:, half_gy:].reshape(-1, NB, NB), quad_places[:half_gx, half_gy:].reshape(-1, KB))
    panels_two, updates_two = lax.map(merge_children, level_two)
    panels_two = panels_two.reshape(half_gx, half_gy, NJ, NS)
    updates_two = updates_two.reshape(half_gx, half_gy, NB, NB)
    return (tiles_out(panels_one, 2, 1), tiles_out(panels_two, 2, 2), tiles_out(updates_two, 2, 2))
```

```python
import functools

import jax
import jax.numpy as jnp
from jax import lax
from jax.experimental import pallas as pl
from jax.experimental.pallas import tpu as pltpu
from jax.sharding import PartitionSpec as P

F32 = jnp.float32
BF16 = jnp.bfloat16
B = 128
NS = 512
NB = 1024
NJ = 1536
LOWER = [(a, b) for a in range(4) for b in range(a + 1)]
VMEM = pl.BlockSpec(memory_space=pltpu.VMEM)
SMEM = pl.BlockSpec(memory_space=pltpu.SMEM)
ANY = pl.BlockSpec(memory_space=pl.ANY)


def full(x):
    return jnp.broadcast_to(x, (8, B))


def split(x):
    hi = x.astype(BF16)
    return hi, (x - hi.astype(F32)).astype(BF16)


def dot3(a, b, dims):
    def one(x, y):
        return lax.dot_general(x, y, (dims, ((), ())), preferred_element_type=F32)

    return (one(a[1], b[0]) + one(a[0], b[1])) + one(a[0], b[0])


NN = ((1,), (0,))
NT = ((1,), (1,))


def factor_block(m):
    for p in range(B // 8):
        r = 8 * p
        x0, x1 = m[r : r + 8, 0:B], m[r : r + 8, B : 2 * B]
        xs = [full(x0[i : i + 1, :]) for i in range(8)]
        ys = [full(x1[i : i + 1, :]) for i in range(8)]
        col = [full(x0[:, r + j : r + j + 1]) for j in range(8)]
        e = [[full(col[j][i : i + 1, :]) if j >= i else None for j in range(8)] for i in range(8)]
        inv = [None] * 8
        for k in range(8):
            inv[k] = lax.rsqrt(e[k][k])
            for j in range(k + 1, 8):
                e[k][j] = e[k][j] * inv[k]
            xs[k], ys[k] = xs[k] * inv[k], ys[k] * inv[k]
            for i in range(k + 1, 8):
                for j in range(i, 8):
                    e[i][j] = e[i][j] - e[k][i] * e[k][j]
                xs[i] = xs[i] - e[k][i] * xs[k]
                ys[i] = ys[i] - e[k][i] * ys[k]
        for k in range(8):
            m[r + k : r + k + 1, 0:B] = xs[k][0:1, :]
            m[r + k : r + k + 1, B : 2 * B] = ys[k][0:1, :]
        for q in range(p + 1, B // 8):
            s = 8 * q
            y0, y1 = m[s : s + 8, 0:B], m[s : s + 8, B : 2 * B]
            c = [full(y0[:, r + j : r + j + 1]) for j in range(8)]
            for k in range(8):
                c[k] = c[k] * inv[k]
                for j in range(k + 1, 8):
                    c[j] = c[j] - c[k] * e[k][j]
                y0 = y0 - c[k] * xs[k]
                y1 = y1 - c[k] * ys[k]
            m[s : s + 8, 0:B] = y0
            m[s : s + 8, B : 2 * B] = y1


def eye_block():
    i0 = lax.broadcasted_iota(jnp.int32, (B, B), 0)
    i1 = lax.broadcasted_iota(jnp.int32, (B, B), 1)
    return i0, i1, jnp.where(i0 == i1, 1.0, 0.0).astype(F32)


def factor_front(g, m, l_ref):
    i0, i1, eye = eye_block()
    m[:, 0:B] = g[0:B, 0:B]
    m[:, B : 2 * B] = eye
    l_ref[...] = jnp.zeros((NS, NS), F32)

    def step(k, carry):
        factor_block(m)
        for kk in range(4):

            @pl.when(k == kk)
            def _(kk=kk):
                c, n = B * kk, B * (kk + 1)
                inverse = m[:, B : 2 * B]
                l_ref[c:n, c:n] = jnp.where(i0 <= i1, m[:, 0:B], 0.0).T
                g[c:n, NS + c : NS + n] = inverse
                inv2 = split(inverse)
                if kk > 0:
                    g[c:n, NS : NS + c] = dot3(inv2, split(g[c:n, NS : NS + c]), NN)
                if kk < 3:
                    right = dot3(inv2, split(g[c:n, n:NS]), NN)
                    below = right.T
                    l_ref[n:NS, c:n] = below
                    below2 = split(below)
                    g[n:NS, n:NS] = g[n:NS, n:NS] - dot3(below2, split(right), NN)
                    m[:, 0:B] = g[n : n + B, n : n + B]
                    m[:, B : 2 * B] = eye
                    g[n:NS, NS : NS + n] = g[n:NS, NS : NS + n] - dot3(below2, split(g[c:n, NS : NS + n]), NN)

        return carry

    lax.fori_loop(0, 4, step, 0)


def solve_rows(bt, g, vt, store):
    inv2 = split(g)
    for h in range(4):
        rows = dot3(split(bt[256 * h : 256 * (h + 1), :]), inv2, NT)
        vt[256 * h : 256 * (h + 1), :] = rows
        store(2 * h, rows[0:B])
        store(2 * h + 1, rows[B : 2 * B])


def order_of(place):
    rank = [sum((place[j] < place[i]).astype(jnp.int32) for j in range(8) if j != i) for i in range(8)]
    return [sum(jnp.where(rank[i] == a, i, 0) for i in range(8)) for a in range(8)]


def source_of(place):
    named, before, result = [], 0, []
    for u in range(8):
        mine = sum((place[i] == 4 + u).astype(jnp.int32) for i in range(8))
        result.append(jnp.where(mine == 1, before, 4 + u - before))
        before = before + mine
    return result


def leaf_solve_kernel(place_ref, leaf, vt, ss, g, m, bt, base, l_buf, sems):
    order = order_of([place_ref[0, i] for i in range(8)])
    at = [pl.multiple_of(NS + B * order[a], B) for a in range(8)]
    first = pltpu.make_async_copy(leaf.at[0:NS, 0:NS], g.at[:, 0:NS], sems.at[0])
    first.start()
    copies = [pltpu.make_async_copy(leaf.at[pl.ds(at[a], B), 0:NS], bt.at[B * a : B * a + B], sems.at[1 + a]) for a in range(8)]
    copies += [
        pltpu.make_async_copy(leaf.at[pl.ds(at[a], B), pl.ds(at[b], B)], base.at[t], sems.at[9 + t])
        for t, (a, b) in enumerate(LOWER)
    ]
    for copy in copies:
        copy.start()
    g[:, NS:NB] = jnp.zeros((NS, NS), F32)
    first.wait()
    factor_front(g, m, l_buf)
    for copy in copies:
        copy.wait()
    solve_rows(bt, g[:, NS:NB], vt, lambda i, rows: None)
    sep_update(vt, ss, lambda t: base[t])


def sep_update(vt, out, base):
    v2 = split(vt[0:NS, :])
    for h in range(2):
        rows = slice(256 * h, 256 * (h + 1))
        prod = dot3((v2[0][rows], v2[1][rows]), (v2[0][0 : 256 * (h + 1)], v2[1][0 : 256 * (h + 1)]), NT)
        for t, (a, b) in enumerate(LOWER):
            if a // 2 == h:
                out[t] = base(t) - prod[B * (a % 2) : B * (a % 2) + B, B * b : B * b + B]


def rest_update(vt, rs, rr, rs_base, rr_base):
    v2 = split(vt[...])
    for h in range(2):
        rows = slice(NS + 256 * h, NS + 256 * (h + 1))
        last = NS + 256 * (h + 1)
        prod = dot3((v2[0][rows], v2[1][rows]), (v2[0][0:last], v2[1][0:last]), NT)
        for a in (2 * h, 2 * h + 1):
            r = B * (a % 2)
            for b in range(4):
                rs[B * a : B * a + B, B * b : B * b + B] = rs_base(a, b) - prod[r : r + B, B * b : B * b + B]
        for t, (a, b) in enumerate(LOWER):
            if a // 2 == h:
                rr[t] = rr_base(t) - prod[B * (a % 2) : B * (a % 2) + B, NS + B * b : NS + B * b + B]


def leaf_rest_kernel(place_ref, leaf, vt, rs, rr, rs_buf, rr_buf, sems):
    order = order_of([place_ref[0, i] for i in range(8)])
    at = [pl.multiple_of(NS + B * order[a], B) for a in range(8)]
    copies = [
        pltpu.make_async_copy(leaf.at[pl.ds(at[4 + a], B), pl.ds(at[b], B)], rs_buf.at[4 * a + b], sems.at[4 * a + b])
        for a in range(4)
        for b in range(4)
    ]
    copies += [
        pltpu.make_async_copy(leaf.at[pl.ds(at[4 + a], B), pl.ds(at[4 + b], B)], rr_buf.at[t], sems.at[16 + t])
        for t, (a, b) in enumerate(LOWER)
    ]
    for copy in copies:
        copy.start()
    for copy in copies:
        copy.wait()
    rest_update(vt, rs, rr, lambda a, b: rs_buf[4 * a + b], lambda t: rr_buf[t])


def leaf_stage(leaf, place):
    vt, ss = pl.pallas_call(
        leaf_solve_kernel,
        out_shape=(jax.ShapeDtypeStruct((NB, NS), F32), jax.ShapeDtypeStruct((10, B, B), F32)),
        in_specs=[SMEM, ANY],
        out_specs=(VMEM, VMEM),
        scratch_shapes=[
            pltpu.VMEM((NS, NB), F32),
            pltpu.VMEM((B, 2 * B), F32),
            pltpu.VMEM((NB, NS), F32),
            pltpu.VMEM((10, B, B), F32),
            pltpu.VMEM((NS, NS), F32),
            pltpu.SemaphoreType.DMA((19,)),
        ],
        cost_estimate=pl.CostEstimate(flops=10**10, bytes_accessed=10**7, transcendentals=0),
        name="leaf_solve",
    )(place, leaf)

    def rest():
        return pl.pallas_call(
            leaf_rest_kernel,
            out_shape=(jax.ShapeDtypeStruct((NS, NS), F32), jax.ShapeDtypeStruct((10, B, B), F32)),
            in_specs=[SMEM, ANY, VMEM],
            out_specs=(VMEM, VMEM),
            scratch_shapes=[pltpu.VMEM((16, B, B), F32), pltpu.VMEM((10, B, B), F32), pltpu.SemaphoreType.DMA((26,))],
            cost_estimate=pl.CostEstimate(flops=3 * 10**9, bytes_accessed=10**7, transcendentals=0),
            name="leaf_rest",
        )(place, leaf, vt)

    return ss, rest


def factor_kernel(own, other, l_ref, inverse, g, m):
    for t, (a, b) in enumerate(LOWER):
        block = own[t] + other[t]
        g[B * a : B * a + B, B * b : B * b + B] = block
        if a != b:
            g[B * b : B * b + B, B * a : B * a + B] = block.T
    g[:, NS:NB] = jnp.zeros((NS, NS), F32)
    factor_front(g, m, l_ref)
    inverse[...] = g[:, NS:NB]


def factor_stage(own, other):
    return pl.pallas_call(
        factor_kernel,
        out_shape=(jax.ShapeDtypeStruct((NS, NS), F32), jax.ShapeDtypeStruct((NS, NS), F32)),
        in_specs=[VMEM, VMEM],
        out_specs=(VMEM, VMEM),
        scratch_shapes=[pltpu.VMEM((NS, NB), F32), pltpu.VMEM((B, 2 * B), F32)],
        cost_estimate=pl.CostEstimate(flops=10**10, bytes_accessed=4 * 10**6, transcendentals=0),
        name="factor",
    )(own, other)


def gather_rows(rs_own, rs_other, source, bt):
    for a in range(8):

        @pl.when(source[a] < 4)
        def _(a=a):
            bt[B * a : B * a + B, :] = rs_own[pl.ds(pl.multiple_of(B * source[a], B), B), :]

        @pl.when(source[a] >= 4)
        def _(a=a):
            bt[B * a : B * a + B, :] = rs_other[pl.ds(pl.multiple_of(B * (source[a] - 4), B), B), :]


def spread_rest(rr_own, rr_other, blocks):
    for h, rr in enumerate((rr_own, rr_other)):
        for t, (a, b) in enumerate(LOWER):
            block = rr[t]
            blocks[16 * h + 4 * a + b] = block
            if a != b:
                blocks[16 * h + 4 * b + a] = block.T
    blocks[32] = jnp.zeros((B, B), F32)


def block_at(source, a, b):
    sa, sb = source[a], source[b]
    same = (sa < 4) == (sb < 4)
    return jnp.where(same, jnp.where(sa < 4, 0, 16) + 4 * (sa % 4) + sb % 4, 32)


def pair_solve_kernel(pair_ref, quad_ref, l_ref, inverse, rs_own, rs_other, rr_own, rr_other, panel, vt, ss, blocks, bt):
    order = order_of([quad_ref[0, i] for i in range(8)])
    where = source_of([pair_ref[0, i] for i in range(8)])
    source = [sum(jnp.where(order[a] == u, where[u], 0) for u in range(8)) for a in range(8)]
    gather_rows(rs_own, rs_other, source, bt)
    panel[0:NS, :] = l_ref[...]

    def store(i, rows):
        panel[pl.ds(pl.multiple_of(NS + B * order[i], B), B), :] = rows

    solve_rows(bt, inverse[...], vt, store)
    spread_rest(rr_own, rr_other, blocks)
    sep_update(vt, ss, lambda t: blocks[block_at(source, *LOWER[t])])


def pair_rest_kernel(pair_ref, quad_ref, vt, rr_own, rr_other, rs, rr, blocks):
    order = order_of([quad_ref[0, i] for i in range(8)])
    where = source_of([pair_ref[0, i] for i in range(8)])
    source = [sum(jnp.where(order[a] == u, where[u], 0) for u in range(8)) for a in range(8)]
    spread_rest(rr_own, rr_other, blocks)
    rest_update(
        vt,
        rs,
        rr,
        lambda a, b: blocks[block_at(source, 4 + a, b)],
        lambda t: blocks[block_at(source, 4 + LOWER[t][0], 4 + LOWER[t][1])],
    )


def pair_stage(pair, quad, l_full, inverse, rs_own, rs_other, rr_own, rr_other):
    panel, vt, ss = pl.pallas_call(
        pair_solve_kernel,
        out_shape=(
            jax.ShapeDtypeStruct((NJ, NS), F32),
            jax.ShapeDtypeStruct((NB, NS), F32),
            jax.ShapeDtypeStruct((10, B, B), F32),
        ),
        in_specs=[SMEM, SMEM] + [VMEM] * 6,
        out_specs=(VMEM,) * 3,
        scratch_shapes=[pltpu.VMEM((33, B, B), F32), pltpu.VMEM((NB, NS), F32)],
        cost_estimate=pl.CostEstimate(flops=3 * 10**9, bytes_accessed=10**7, transcendentals=0),
        name="pair_solve",
    )(pair, quad, l_full, inverse, rs_own, rs_other, rr_own, rr_other)

    def rest():
        return pl.pallas_call(
            pair_rest_kernel,
            out_shape=(jax.ShapeDtypeStruct((NS, NS), F32), jax.ShapeDtypeStruct((10, B, B), F32)),
            in_specs=[SMEM, SMEM] + [VMEM] * 3,
            out_specs=(VMEM, VMEM),
            scratch_shapes=[pltpu.VMEM((33, B, B), F32)],
            cost_estimate=pl.CostEstimate(flops=3 * 10**9, bytes_accessed=10**7, transcendentals=0),
            name="pair_rest",
        )(pair, quad, vt, rr_own, rr_other)

    return panel, ss, rest


def quad_kernel(quad_ref, l_ref, inverse, rs_own, rs_other, rr_own, rr_other, panel, update, blocks, bt, vt):
    source = source_of([quad_ref[0, i] for i in range(8)])
    gather_rows(rs_own, rs_other, source, bt)
    panel[0:NS, :] = l_ref[...]

    def store(i, rows):
        panel[NS + B * i : NS + B * i + B, :] = rows

    solve_rows(bt, inverse[...], vt, store)
    spread_rest(rr_own, rr_other, blocks)
    v2 = split(vt[...])
    for h in range(4):
        rows = slice(256 * h, 256 * (h + 1))
        last = 256 * (h + 1)
        prod = dot3((v2[0][rows], v2[1][rows]), (v2[0][0:last], v2[1][0:last]), NT)
        for a in (2 * h, 2 * h + 1):
            r = B * (a % 2)
            for b in range(a + 1):
                block = blocks[block_at(source, a, b)] - prod[r : r + B, B * b : B * b + B]
                update[B * a : B * a + B, B * b : B * b + B] = block
                if a != b:
                    update[B * b : B * b + B, B * a : B * a + B] = block.T


def quad_stage(quad, l_full, inverse, rs_own, rs_other, rr_own, rr_other):
    return pl.pallas_call(
        quad_kernel,
        out_shape=(jax.ShapeDtypeStruct((NJ, NS), F32), jax.ShapeDtypeStruct((NB, NB), F32)),
        in_specs=[SMEM] + [VMEM] * 6,
        out_specs=(VMEM, VMEM),
        scratch_shapes=[pltpu.VMEM((33, B, B), F32), pltpu.VMEM((NB, NS), F32), pltpu.VMEM((NB, NS), F32)],
        cost_estimate=pl.CostEstimate(flops=4 * 10**9, bytes_accessed=10**7, transcendentals=0),
        name="quad",
    )(quad, l_full, inverse, rs_own, rs_other, rr_own, rr_other)


def swapped(value, axis):
    size = lax.axis_size(axis)
    return lax.ppermute(value, axis, [(i, (i + size // 2) % size) for i in range(size)])


def exchange(ss, rest, axis):
    other_ss = swapped(ss, axis)
    rs, rr = rest()
    other_ss, rs_late, rr_late = lax.optimization_barrier((other_ss, rs, rr))
    return other_ss, rs, rr, swapped(rs_late, axis), swapped(rr_late, axis)


def shards(leaf_front, place_pairs, place_quads):
    ss, rest = leaf_stage(leaf_front, place_pairs)
    other_ss, rs, rr, other_rs, other_rr = exchange(ss, rest, "gx")
    l_pair, inverse = factor_stage(ss, other_ss)
    pair_panel, ss, rest = pair_stage(place_pairs, place_quads, l_pair, inverse, rs, other_rs, rr, other_rr)
    other_ss, rs, rr, other_rs, other_rr = exchange(ss, rest, "gy")
    l_quad, inverse = factor_stage(ss, other_ss)
    quad_panel, quad_update = quad_stage(place_quads, l_quad, inverse, rs, other_rs, rr, other_rr)
    return pair_panel, quad_panel, quad_update


def solution(mesh):
    spec = P("gx", "gy")
    return jax.shard_map(shards, mesh=mesh, in_specs=(spec,) * 3, out_specs=(spec,) * 3, check_vma=False)
```

```python
import functools

import jax
import jax.numpy as jnp
from jax import lax
from jax.experimental import pallas as pl
from jax.experimental.pallas import tpu as pltpu
from jax.sharding import PartitionSpec as P

F32 = jnp.float32
BF16 = jnp.bfloat16
B = 128
NS = 512
NB = 1024
NJ = 1536
LOWER = [(a, b) for a in range(4) for b in range(a + 1)]
VMEM = pl.BlockSpec(memory_space=pltpu.VMEM)
SMEM = pl.BlockSpec(memory_space=pltpu.SMEM)
ANY = pl.BlockSpec(memory_space=pltpu.HBM)


def full(x):
    return jnp.broadcast_to(x, (8, B))


def split(x):
    hi = x.astype(BF16)
    return hi, (x - hi.astype(F32)).astype(BF16)


def dot3(a, b, dims):
    def one(x, y):
        return lax.dot_general(x, y, (dims, ((), ())), preferred_element_type=F32)

    return (one(a[1], b[0]) + one(a[0], b[1])) + one(a[0], b[0])


NN = ((1,), (0,))
NT = ((1,), (1,))


def factor_block(m):
    for p in range(B // 8):
        r = 8 * p
        x0, x1 = m[r : r + 8, 0:B], m[r : r + 8, B : 2 * B]
        xs = [full(x0[i : i + 1, :]) for i in range(8)]
        ys = [full(x1[i : i + 1, :]) for i in range(8)]
        col = [full(x0[:, r + j : r + j + 1]) for j in range(8)]
        e = [[full(col[j][i : i + 1, :]) if j >= i else None for j in range(8)] for i in range(8)]
        inv = [None] * 8
        for k in range(8):
            inv[k] = lax.rsqrt(e[k][k])
            for j in range(k + 1, 8):
                e[k][j] = e[k][j] * inv[k]
            xs[k], ys[k] = xs[k] * inv[k], ys[k] * inv[k]
            for i in range(k + 1, 8):
                for j in range(i, 8):
                    e[i][j] = e[i][j] - e[k][i] * e[k][j]
                xs[i] = xs[i] - e[k][i] * xs[k]
                ys[i] = ys[i] - e[k][i] * ys[k]
        for k in range(8):
            m[r + k : r + k + 1, 0:B] = xs[k][0:1, :]
            m[r + k : r + k + 1, B : 2 * B] = ys[k][0:1, :]
        for q in range(p + 1, B // 8):
            s = 8 * q
            y0, y1 = m[s : s + 8, 0:B], m[s : s + 8, B : 2 * B]
            c = [full(y0[:, r + j : r + j + 1]) for j in range(8)]
            for k in range(8):
                c[k] = c[k] * inv[k]
                for j in range(k + 1, 8):
                    c[j] = c[j] - c[k] * e[k][j]
                y0 = y0 - c[k] * xs[k]
                y1 = y1 - c[k] * ys[k]
            m[s : s + 8, 0:B] = y0
            m[s : s + 8, B : 2 * B] = y1


def eye_block():
    i0 = lax.broadcasted_iota(jnp.int32, (B, B), 0)
    i1 = lax.broadcasted_iota(jnp.int32, (B, B), 1)
    return i0, i1, jnp.where(i0 == i1, 1.0, 0.0).astype(F32)


def factor_front(g, m, l_ref):
    i0, i1, eye = eye_block()
    m[:, 0:B] = g[0:B, 0:B]
    m[:, B : 2 * B] = eye
    l_ref[...] = jnp.zeros((NS, NS), F32)

    def step(k, carry):
        factor_block(m)
        for kk in range(4):

            @pl.when(k == kk)
            def _(kk=kk):
                c, n = B * kk, B * (kk + 1)
                inverse = m[:, B : 2 * B]
                l_ref[c:n, c:n] = jnp.where(i0 <= i1, m[:, 0:B], 0.0).T
                g[c:n, NS + c : NS + n] = inverse
                inv2 = split(inverse)
                if kk > 0:
                    g[c:n, NS : NS + c] = dot3(inv2, split(g[c:n, NS : NS + c]), NN)
                if kk < 3:
                    right = dot3(inv2, split(g[c:n, n:NS]), NN)
                    below = right.T
                    l_ref[n:NS, c:n] = below
                    below2 = split(below)
                    g[n:NS, n:NS] = g[n:NS, n:NS] - dot3(below2, split(right), NN)
                    m[:, 0:B] = g[n : n + B, n : n + B]
                    m[:, B : 2 * B] = eye
                    g[n:NS, NS : NS + n] = g[n:NS, NS : NS + n] - dot3(below2, split(g[c:n, NS : NS + n]), NN)

        return carry

    lax.fori_loop(0, 4, step, 0)


def solve_rows(bt, g, vt, store):
    inv2 = split(g)
    for h in range(4):
        rows = dot3(split(bt[256 * h : 256 * (h + 1), :]), inv2, NT)
        vt[256 * h : 256 * (h + 1), :] = rows
        store(2 * h, rows[0:B])
        store(2 * h + 1, rows[B : 2 * B])


def order_of(place):
    rank = [sum((place[j] < place[i]).astype(jnp.int32) for j in range(8) if j != i) for i in range(8)]
    return [sum(jnp.where(rank[i] == a, i, 0) for i in range(8)) for a in range(8)]


def source_of(place):
    named, before, result = [], 0, []
    for u in range(8):
        mine = sum((place[i] == 4 + u).astype(jnp.int32) for i in range(8))
        result.append(jnp.where(mine == 1, before, 4 + u - before))
        before = before + mine
    return result


def leaf_solve_kernel(place_ref, leaf, vt, ss, g, m, bt, base, l_buf, sems):
    order = order_of([place_ref[0, i] for i in range(8)])
    at = [pl.multiple_of(NS + B * order[a], B) for a in range(8)]
    first = pltpu.make_async_copy(leaf.at[0:NS, 0:NS], g.at[:, 0:NS], sems.at[0])
    first.start()
    copies = [pltpu.make_async_copy(leaf.at[pl.ds(at[a], B), 0:NS], bt.at[B * a : B * a + B], sems.at[1 + a]) for a in range(8)]
    copies += [
        pltpu.make_async_copy(leaf.at[pl.ds(at[a], B), pl.ds(at[b], B)], base.at[t], sems.at[9 + t])
        for t, (a, b) in enumerate(LOWER)
    ]
    for copy in copies:
        copy.start()
    g[:, NS:NB] = jnp.zeros((NS, NS), F32)
    first.wait()
    factor_front(g, m, l_buf)
    for copy in copies:
        copy.wait()
    solve_rows(bt, g[:, NS:NB], vt, lambda i, rows: None)
    sep_product(split(vt[0:NS, :]), setter(ss, lambda t, block: base[t] - block))


def sep_product(v2, put):
    for h in range(2):
        rows = slice(256 * h, 256 * (h + 1))
        prod = dot3((v2[0][rows], v2[1][rows]), (v2[0][0 : 256 * (h + 1)], v2[1][0 : 256 * (h + 1)]), NT)
        for t, (a, b) in enumerate(LOWER):
            if a // 2 == h:
                put(t, prod[B * (a % 2) : B * (a % 2) + B, B * b : B * b + B])


def rest_product(v2, put_rs, put_rr):
    for h in range(2):
        rows = slice(NS + 256 * h, NS + 256 * (h + 1))
        last = NS + 256 * (h + 1)
        prod = dot3((v2[0][rows], v2[1][rows]), (v2[0][0:last], v2[1][0:last]), NT)
        for a in (2 * h, 2 * h + 1):
            r = B * (a % 2)
            for b in range(4):
                put_rs(a, b, prod[r : r + B, B * b : B * b + B])
        for t, (a, b) in enumerate(LOWER):
            if a // 2 == h:
                put_rr(t, prod[B * (a % 2) : B * (a % 2) + B, NS + B * b : NS + B * b + B])


def setter(ref, value):
    def put(t, block):
        ref[t] = value(t, block)

    return put


def rs_setter(ref, value):
    def put(a, b, block):
        ref[B * a : B * a + B, B * b : B * b + B] = value(a, b, block)

    return put


def leaf_rest_kernel(place_ref, leaf, vt, rs, rr, rs_buf, rr_buf, sems):
    order = order_of([place_ref[0, i] for i in range(8)])
    at = [pl.multiple_of(NS + B * order[a], B) for a in range(8)]
    copies = [
        pltpu.make_async_copy(leaf.at[pl.ds(at[4 + a], B), pl.ds(at[b], B)], rs_buf.at[4 * a + b], sems.at[4 * a + b])
        for a in range(4)
        for b in range(4)
    ]
    copies += [
        pltpu.make_async_copy(leaf.at[pl.ds(at[4 + a], B), pl.ds(at[4 + b], B)], rr_buf.at[t], sems.at[16 + t])
        for t, (a, b) in enumerate(LOWER)
    ]
    for copy in copies:
        copy.start()
    for copy in copies:
        copy.wait()
    rest_product(
        split(vt[...]),
        rs_setter(rs, lambda a, b, block: rs_buf[4 * a + b] - block),
        setter(rr, lambda t, block: rr_buf[t] - block),
    )


def leaf_stage(leaf, place):
    vt, ss = pl.pallas_call(
        leaf_solve_kernel,
        out_shape=(jax.ShapeDtypeStruct((NB, NS), F32), jax.ShapeDtypeStruct((10, B, B), F32)),
        in_specs=[SMEM, ANY],
        out_specs=(VMEM, VMEM),
        scratch_shapes=[
            pltpu.VMEM((NS, NB), F32),
            pltpu.VMEM((B, 2 * B), F32),
            pltpu.VMEM((NB, NS), F32),
            pltpu.VMEM((10, B, B), F32),
            pltpu.VMEM((NS, NS), F32),
            pltpu.SemaphoreType.DMA((19,)),
        ],
        cost_estimate=pl.CostEstimate(flops=10**10, bytes_accessed=10**7, transcendentals=0),
        compiler_params=pltpu.CompilerParams(vmem_limit_bytes=54 * 2**20),
        name="leaf_solve",
    )(place, leaf)

    def rest():
        return pl.pallas_call(
            leaf_rest_kernel,
            out_shape=(jax.ShapeDtypeStruct((NS, NS), F32), jax.ShapeDtypeStruct((10, B, B), F32)),
            in_specs=[SMEM, ANY, VMEM],
            out_specs=(VMEM, VMEM),
            scratch_shapes=[pltpu.VMEM((16, B, B), F32), pltpu.VMEM((10, B, B), F32), pltpu.SemaphoreType.DMA((26,))],
            cost_estimate=pl.CostEstimate(flops=3 * 10**9, bytes_accessed=10**7, transcendentals=0),
            compiler_params=pltpu.CompilerParams(vmem_limit_bytes=54 * 2**20),
            name="leaf_rest",
        )(place, leaf, vt)

    return ss, rest


def factor_kernel(own, other, l_ref, inverse, g, m):
    for t, (a, b) in enumerate(LOWER):
        block = own[t] + other[t]
        g[B * a : B * a + B, B * b : B * b + B] = block
        if a != b:
            g[B * b : B * b + B, B * a : B * a + B] = block.T
    g[:, NS:NB] = jnp.zeros((NS, NS), F32)
    factor_front(g, m, l_ref)
    inverse[...] = g[:, NS:NB]


def factor_stage(own, other):
    return pl.pallas_call(
        factor_kernel,
        out_shape=(jax.ShapeDtypeStruct((NS, NS), F32), jax.ShapeDtypeStruct((NS, NS), F32)),
        in_specs=[VMEM, VMEM],
        out_specs=(VMEM, VMEM),
        scratch_shapes=[pltpu.VMEM((NS, NB), F32), pltpu.VMEM((B, 2 * B), F32)],
        cost_estimate=pl.CostEstimate(flops=10**10, bytes_accessed=4 * 10**6, transcendentals=0),
        compiler_params=pltpu.CompilerParams(vmem_limit_bytes=16 * 2**20),
        name="factor",
    )(own, other)


def gather_rows(rs_own, rs_other, source, bt):
    for a in range(8):

        @pl.when(source[a] < 4)
        def _(a=a):
            bt[B * a : B * a + B, :] = rs_own[pl.ds(pl.multiple_of(B * source[a], B), B), :]

        @pl.when(source[a] >= 4)
        def _(a=a):
            bt[B * a : B * a + B, :] = rs_other[pl.ds(pl.multiple_of(B * (source[a] - 4), B), B), :]


def spread_rest(rr_own, rr_other, blocks):
    for h, rr in enumerate((rr_own, rr_other)):
        for t, (a, b) in enumerate(LOWER):
            block = rr[t]
            blocks[16 * h + 4 * a + b] = block
            if a != b:
                blocks[16 * h + 4 * b + a] = block.T
    blocks[32] = jnp.zeros((B, B), F32)


def block_at(source, a, b):
    sa, sb = source[a], source[b]
    same = (sa < 4) == (sb < 4)
    return jnp.where(same, jnp.where(sa < 4, 0, 16) + 4 * (sa % 4) + sb % 4, 32)


def pair_order(pair_ref, quad_ref):
    order = order_of([quad_ref[0, i] for i in range(8)])
    where = source_of([pair_ref[0, i] for i in range(8)])
    return order, [sum(jnp.where(order[a] == u, where[u], 0) for u in range(8)) for a in range(8)]


def pair_solve_kernel(pair_ref, quad_ref, l_ref, inverse, rs_own, rs_other, panel, ss, rs, rr, bt, vt):
    order, source = pair_order(pair_ref, quad_ref)
    gather_rows(rs_own, rs_other, source, bt)
    panel[0:NS, :] = l_ref[...]

    def store(i, rows):
        panel[pl.ds(pl.multiple_of(NS + B * order[i], B), B), :] = rows

    solve_rows(bt, inverse[...], vt, store)
    v2 = split(vt[...])
    sep_product(v2, setter(ss, lambda t, block: block))
    rest_product(v2, rs_setter(rs, lambda a, b, block: block), setter(rr, lambda t, block: block))


def pair_update_kernel(pair_ref, quad_ref, ss_in, rs_in, rr_in, rr_own, rr_other, ss, rs, rr, blocks):
    _, source = pair_order(pair_ref, quad_ref)
    spread_rest(rr_own, rr_other, blocks)
    for t, (a, b) in enumerate(LOWER):
        ss[t] = blocks[block_at(source, a, b)] - ss_in[t]
        rr[t] = blocks[block_at(source, 4 + a, 4 + b)] - rr_in[t]
    for a in range(4):
        for b in range(4):
            at = (slice(B * a, B * a + B), slice(B * b, B * b + B))
            rs[at] = blocks[block_at(source, 4 + a, b)] - rs_in[at]


LOWER10 = jax.ShapeDtypeStruct((10, B, B), F32)
SQUARE = jax.ShapeDtypeStruct((NS, NS), F32)
PANEL = jax.ShapeDtypeStruct((NJ, NS), F32)


def params(mib):
    return pltpu.CompilerParams(vmem_limit_bytes=mib * 2**20)


def pair_stage(pair, quad, l_full, inverse, rs_own, rs_other, rr_own, rr_other):
    panel, ss, rs, rr = pl.pallas_call(
        pair_solve_kernel,
        out_shape=(PANEL, LOWER10, SQUARE, LOWER10),
        in_specs=[SMEM, SMEM] + [VMEM] * 4,
        out_specs=(VMEM,) * 4,
        scratch_shapes=[pltpu.VMEM((NB, NS), F32), pltpu.VMEM((NB, NS), F32)],
        compiler_params=params(32),
        cost_estimate=pl.CostEstimate(flops=3 * 10**9, bytes_accessed=10**7, transcendentals=0),
        name="pair_solve",
    )(pair, quad, l_full, inverse, rs_own, rs_other)
    ss, rs, rr = pl.pallas_call(
        pair_update_kernel,
        out_shape=(LOWER10, SQUARE, LOWER10),
        in_specs=[SMEM, SMEM] + [VMEM] * 5,
        out_specs=(VMEM,) * 3,
        scratch_shapes=[pltpu.VMEM((33, B, B), F32)],
        compiler_params=params(24),
        cost_estimate=pl.CostEstimate(flops=10**6, bytes_accessed=10**7, transcendentals=0),
        name="pair_update",
    )(pair, quad, ss, rs, rr, rr_own, rr_other)
    return panel, ss, rs, rr


def quad_solve_kernel(quad_ref, l_ref, inverse, rs_own, rs_other, panel, lower, bt, vt):
    source = source_of([quad_ref[0, i] for i in range(8)])
    gather_rows(rs_own, rs_other, source, bt)
    panel[0:NS, :] = l_ref[...]

    def store(i, rows):
        panel[NS + B * i : NS + B * i + B, :] = rows

    solve_rows(bt, inverse[...], vt, store)
    v2 = split(vt[...])
    for h in range(4):
        rows = slice(256 * h, 256 * (h + 1))
        last = 256 * (h + 1)
        lower[rows, 0:last] = dot3((v2[0][rows], v2[1][rows]), (v2[0][0:last], v2[1][0:last]), NT)


def quad_update_kernel(quad_ref, lower, rr_own, rr_other, update, blocks):
    source = source_of([quad_ref[0, i] for i in range(8)])
    spread_rest(rr_own, rr_other, blocks)
    for a in range(8):
        for b in range(a + 1):
            block = blocks[block_at(source, a, b)] - lower[B * a : B * a + B, B * b : B * b + B]
            update[B * a : B * a + B, B * b : B * b + B] = block
            if a != b:
                update[B * b : B * b + B, B * a : B * a + B] = block.T


def quad_stage(quad, l_full, inverse, rs_own, rs_other, rr_own, rr_other):
    panel, lower = pl.pallas_call(
        quad_solve_kernel,
        out_shape=(PANEL, jax.ShapeDtypeStruct((NB, NB), F32)),
        in_specs=[SMEM] + [VMEM] * 4,
        out_specs=(VMEM, VMEM),
        scratch_shapes=[pltpu.VMEM((NB, NS), F32), pltpu.VMEM((NB, NS), F32)],
        compiler_params=params(32),
        cost_estimate=pl.CostEstimate(flops=4 * 10**9, bytes_accessed=10**7, transcendentals=0),
        name="quad_solve",
    )(quad, l_full, inverse, rs_own, rs_other)
    update = pl.pallas_call(
        quad_update_kernel,
        out_shape=jax.ShapeDtypeStruct((NB, NB), F32),
        in_specs=[SMEM] + [VMEM] * 3,
        out_specs=VMEM,
        scratch_shapes=[pltpu.VMEM((33, B, B), F32)],
        compiler_params=params(24),
        cost_estimate=pl.CostEstimate(flops=10**6, bytes_accessed=10**7, transcendentals=0),
        name="quad_update",
    )(quad, lower, rr_own, rr_other)
    return panel, update


def swapped(value, axis):
    size = lax.axis_size(axis)
    return lax.ppermute(value, axis, [(i, (i + size // 2) % size) for i in range(size)])


def shards(leaf_front, place_pairs, place_quads):
    ss, rest = leaf_stage(leaf_front, place_pairs)
    other_ss = swapped(ss, "gx")
    rs, rr = rest()
    other_rs, other_rr = swapped(rs, "gx"), swapped(rr, "gx")
    l_pair, inverse = factor_stage(ss, other_ss)
    pair_panel, ss, rs, rr = pair_stage(place_pairs, place_quads, l_pair, inverse, rs, other_rs, rr, other_rr)
    other_ss, other_rs, other_rr = swapped(ss, "gy"), swapped(rs, "gy"), swapped(rr, "gy")
    l_quad, inverse = factor_stage(ss, other_ss)
    quad_panel, quad_update = quad_stage(place_quads, l_quad, inverse, rs, other_rs, rr, other_rr)
    return pair_panel, quad_panel, quad_update


def solution(mesh):
    spec = P("gx", "gy")
    return jax.shard_map(shards, mesh=mesh, in_specs=(spec,) * 3, out_specs=(spec,) * 3, check_vma=False)
```

```python
import functools

import jax
import jax.numpy as jnp
from jax import lax
from jax.experimental import pallas as pl
from jax.experimental.pallas import tpu as pltpu
from jax.sharding import PartitionSpec as P

F32 = jnp.float32
BF16 = jnp.bfloat16
B = 128
NS = 512
NB = 1024
NJ = 1536
LOWER = [(a, b) for a in range(4) for b in range(a + 1)]
VMEM = pl.BlockSpec(memory_space=pltpu.VMEM)
MESH = pl.DeviceIdType.MESH
RS0, RR0, BLOCKS = 10, 26, 36
CHUNKS = [(2 * i, 2) for i in range(5)] + [(RS0 + 4 * i, 4) for i in range(4)] + [(RR0, 4), (RR0 + 4, 6)]
SEP_CHUNKS = 5
FORWARD = [(5, 6, 7), (8, 9), (10,), ()]
SMEM = pl.BlockSpec(memory_space=pltpu.SMEM)
ANY = pl.BlockSpec(memory_space=pltpu.HBM)


def full(x):
    return jnp.broadcast_to(x, (8, B))


def split(x):
    hi = x.astype(BF16)
    return hi, (x - hi.astype(F32)).astype(BF16)


def dot3(a, b, dims):
    def one(x, y):
        return lax.dot_general(x, y, (dims, ((), ())), preferred_element_type=F32)

    return (one(a[1], b[0]) + one(a[0], b[1])) + one(a[0], b[0])


NN = ((1,), (0,))
NT = ((1,), (1,))


def factor_block(m):
    for p in range(B // 8):
        r = 8 * p
        x0, x1 = m[r : r + 8, 0:B], m[r : r + 8, B : 2 * B]
        xs = [full(x0[i : i + 1, :]) for i in range(8)]
        ys = [full(x1[i : i + 1, :]) for i in range(8)]
        col = [full(x0[:, r + j : r + j + 1]) for j in range(8)]
        e = [[full(col[j][i : i + 1, :]) if j >= i else None for j in range(8)] for i in range(8)]
        inv = [None] * 8
        for k in range(8):
            inv[k] = lax.rsqrt(e[k][k])
            for j in range(k + 1, 8):
                e[k][j] = e[k][j] * inv[k]
            xs[k], ys[k] = xs[k] * inv[k], ys[k] * inv[k]
            for i in range(k + 1, 8):
                for j in range(i, 8):
                    e[i][j] = e[i][j] - e[k][i] * e[k][j]
                xs[i] = xs[i] - e[k][i] * xs[k]
                ys[i] = ys[i] - e[k][i] * ys[k]
        for k in range(8):
            m[r + k : r + k + 1, 0:B] = xs[k][0:1, :]
            m[r + k : r + k + 1, B : 2 * B] = ys[k][0:1, :]
        for q in range(p + 1, B // 8):
            s = 8 * q
            y0, y1 = m[s : s + 8, 0:B], m[s : s + 8, B : 2 * B]
            c = [full(y0[:, r + j : r + j + 1]) for j in range(8)]
            for k in range(8):
                c[k] = c[k] * inv[k]
                for j in range(k + 1, 8):
                    c[j] = c[j] - c[k] * e[k][j]
                y0 = y0 - c[k] * xs[k]
                y1 = y1 - c[k] * ys[k]
            m[s : s + 8, 0:B] = y0
            m[s : s + 8, B : 2 * B] = y1


def eye_block():
    i0 = lax.broadcasted_iota(jnp.int32, (B, B), 0)
    i1 = lax.broadcasted_iota(jnp.int32, (B, B), 1)
    return i0, i1, jnp.where(i0 == i1, 1.0, 0.0).astype(F32)


def factor_front(g, m, l_ref, after=lambda step: None):
    i0, i1, eye = eye_block()
    m[:, 0:B] = g[0:B, 0:B]
    m[:, B : 2 * B] = eye
    l_ref[...] = jnp.zeros((NS, NS), F32)

    def step(k, carry):
        factor_block(m)
        for kk in range(4):

            @pl.when(k == kk)
            def _(kk=kk):
                after(kk)
                c, n = B * kk, B * (kk + 1)
                inverse = m[:, B : 2 * B]
                l_ref[c:n, c:n] = jnp.where(i0 <= i1, m[:, 0:B], 0.0).T
                g[c:n, NS + c : NS + n] = inverse
                inv2 = split(inverse)
                if kk > 0:
                    g[c:n, NS : NS + c] = dot3(inv2, split(g[c:n, NS : NS + c]), NN)
                if kk < 3:
                    right = dot3(inv2, split(g[c:n, n:NS]), NN)
                    below = right.T
                    l_ref[n:NS, c:n] = below
                    below2 = split(below)
                    g[n:NS, n:NS] = g[n:NS, n:NS] - dot3(below2, split(right), NN)
                    m[:, 0:B] = g[n : n + B, n : n + B]
                    m[:, B : 2 * B] = eye
                    g[n:NS, NS : NS + n] = g[n:NS, NS : NS + n] - dot3(below2, split(g[c:n, NS : NS + n]), NN)

        return carry

    lax.fori_loop(0, 4, step, 0)


def solve_rows(bt, g, vt, store):
    inv2 = split(g)
    for h in range(4):
        rows = dot3(split(bt[256 * h : 256 * (h + 1), :]), inv2, NT)
        vt[256 * h : 256 * (h + 1), :] = rows
        store(2 * h, rows[0:B])
        store(2 * h + 1, rows[B : 2 * B])


def order_of(place):
    rank = [sum((place[j] < place[i]).astype(jnp.int32) for j in range(8) if j != i) for i in range(8)]
    return [sum(jnp.where(rank[i] == a, i, 0) for i in range(8)) for a in range(8)]


def source_of(place):
    named, before, result = [], 0, []
    for u in range(8):
        mine = sum((place[i] == 4 + u).astype(jnp.int32) for i in range(8))
        result.append(jnp.where(mine == 1, before, 4 + u - before))
        before = before + mine
    return result


def leaf_solve_kernel(place_ref, leaf, vt, ss, g, m, bt, base, l_buf, sems):
    order = order_of([place_ref[0, i] for i in range(8)])
    at = [pl.multiple_of(NS + B * order[a], B) for a in range(8)]
    first = pltpu.make_async_copy(leaf.at[0:NS, 0:NS], g.at[:, 0:NS], sems.at[0])
    first.start()
    copies = [pltpu.make_async_copy(leaf.at[pl.ds(at[a], B), 0:NS], bt.at[B * a : B * a + B], sems.at[1 + a]) for a in range(8)]
    copies += [
        pltpu.make_async_copy(leaf.at[pl.ds(at[a], B), pl.ds(at[b], B)], base.at[t], sems.at[9 + t])
        for t, (a, b) in enumerate(LOWER)
    ]
    for copy in copies:
        copy.start()
    g[:, NS:NB] = jnp.zeros((NS, NS), F32)
    first.wait()
    factor_front(g, m, l_buf)
    for copy in copies:
        copy.wait()
    solve_rows(bt, g[:, NS:NB], vt, lambda i, rows: None)
    sep_product(split(vt[0:NS, :]), setter(ss, lambda t, block: base[t] - block))


def sep_product(v2, put):
    for h in range(2):
        rows = slice(256 * h, 256 * (h + 1))
        prod = dot3((v2[0][rows], v2[1][rows]), (v2[0][0 : 256 * (h + 1)], v2[1][0 : 256 * (h + 1)]), NT)
        for t, (a, b) in enumerate(LOWER):
            if a // 2 == h:
                put(t, prod[B * (a % 2) : B * (a % 2) + B, B * b : B * b + B])


def rest_product(v2, put_rs, put_rr):
    for h in range(2):
        rows = slice(NS + 256 * h, NS + 256 * (h + 1))
        last = NS + 256 * (h + 1)
        prod = dot3((v2[0][rows], v2[1][rows]), (v2[0][0:last], v2[1][0:last]), NT)
        for a in (2 * h, 2 * h + 1):
            r = B * (a % 2)
            for b in range(4):
                put_rs(a, b, prod[r : r + B, B * b : B * b + B])
        for t, (a, b) in enumerate(LOWER):
            if a // 2 == h:
                put_rr(t, prod[B * (a % 2) : B * (a % 2) + B, NS + B * b : NS + B * b + B])


def setter(ref, value):
    def put(t, block):
        ref[t] = value(t, block)

    return put


def rs_setter(ref, value):
    def put(a, b, block):
        ref[B * a : B * a + B, B * b : B * b + B] = value(a, b, block)

    return put


def leaf_rest_kernel(place_ref, leaf, vt, rs, rr, rs_buf, rr_buf, sems):
    order = order_of([place_ref[0, i] for i in range(8)])
    at = [pl.multiple_of(NS + B * order[a], B) for a in range(8)]
    copies = [
        pltpu.make_async_copy(leaf.at[pl.ds(at[4 + a], B), pl.ds(at[b], B)], rs_buf.at[4 * a + b], sems.at[4 * a + b])
        for a in range(4)
        for b in range(4)
    ]
    copies += [
        pltpu.make_async_copy(leaf.at[pl.ds(at[4 + a], B), pl.ds(at[4 + b], B)], rr_buf.at[t], sems.at[16 + t])
        for t, (a, b) in enumerate(LOWER)
    ]
    for copy in copies:
        copy.start()
    for copy in copies:
        copy.wait()
    rest_product(
        split(vt[...]),
        rs_setter(rs, lambda a, b, block: rs_buf[4 * a + b] - block),
        setter(rr, lambda t, block: rr_buf[t] - block),
    )


def leaf_stage(leaf, place):
    vt, ss = pl.pallas_call(
        leaf_solve_kernel,
        out_shape=(jax.ShapeDtypeStruct((NB, NS), F32), jax.ShapeDtypeStruct((10, B, B), F32)),
        in_specs=[SMEM, ANY],
        out_specs=(VMEM, VMEM),
        scratch_shapes=[
            pltpu.VMEM((NS, NB), F32),
            pltpu.VMEM((B, 2 * B), F32),
            pltpu.VMEM((NB, NS), F32),
            pltpu.VMEM((10, B, B), F32),
            pltpu.VMEM((NS, NS), F32),
            pltpu.SemaphoreType.DMA((19,)),
        ],
        cost_estimate=pl.CostEstimate(flops=10**10, bytes_accessed=10**7, transcendentals=0),
        compiler_params=pltpu.CompilerParams(vmem_limit_bytes=54 * 2**20),
        name="leaf_solve",
    )(place, leaf)

    def rest():
        return pl.pallas_call(
            leaf_rest_kernel,
            out_shape=(jax.ShapeDtypeStruct((NS, NS), F32), jax.ShapeDtypeStruct((10, B, B), F32)),
            in_specs=[SMEM, ANY, VMEM],
            out_specs=(VMEM, VMEM),
            scratch_shapes=[pltpu.VMEM((16, B, B), F32), pltpu.VMEM((10, B, B), F32), pltpu.SemaphoreType.DMA((26,))],
            cost_estimate=pl.CostEstimate(flops=3 * 10**9, bytes_accessed=10**7, transcendentals=0),
            compiler_params=pltpu.CompilerParams(vmem_limit_bytes=54 * 2**20),
            name="leaf_rest",
        )(place, leaf, vt)

    return ss, rest


def factor_kernel(own, other, l_ref, inverse, g, m):
    joined_separator(own, other, g)
    factor_front(g, m, l_ref)
    inverse[...] = g[:, NS:NB]


def joined_separator(own, other, g):
    for t, (a, b) in enumerate(LOWER):
        block = own[t] + other[t]
        g[B * a : B * a + B, B * b : B * b + B] = block
        if a != b:
            g[B * b : B * b + B, B * a : B * a + B] = block.T
    g[:, NS:NB] = jnp.zeros((NS, NS), F32)


def quad_factor_kernel(half_gx, half_gy, own, l_ref, inverse, received, other, g, m, far_send, far_recv, near_send, near_recv):
    gx, gy = lax.axis_index("gx"), lax.axis_index("gy")
    side = gx // half_gx
    far = (gx, lax.rem(gy + half_gy, 2 * half_gy))
    near = (lax.rem(gx + half_gx, 2 * half_gx), gy)
    barrier = pltpu.get_barrier_semaphore()
    for device in (far, near):
        pl.semaphore_signal(barrier, inc=1, device_id=device, device_id_type=MESH)
    pl.semaphore_wait(barrier, 2)

    def far_copy(c):
        start, count = CHUNKS[c]
        part = pl.ds(start + side * (count // 2), count // 2)
        return pltpu.make_async_remote_copy(
            own.at[part], other.at[part], far_send.at[c], far_recv.at[c], device_id=far, device_id_type=MESH
        )

    def near_copy(c):
        start, count = CHUNKS[c]
        part = pl.ds(start + side * (count // 2), count // 2)
        return pltpu.make_async_remote_copy(
            other.at[part], other.at[part], near_send.at[c], near_recv.at[c], device_id=near, device_id_type=MESH
        )

    def forward(c):
        far_copy(c).wait_recv()
        near_copy(c).start()

    for c in range(len(CHUNKS)):
        far_copy(c).start()
    for c in range(SEP_CHUNKS):
        forward(c)
    for c in range(SEP_CHUNKS):
        near_copy(c).wait_recv()
    joined_separator(own, other, g)

    def after(step):
        for c in FORWARD[step]:
            forward(c)

    factor_front(g, m, l_ref, after)
    inverse[...] = g[:, NS:NB]
    for c in range(len(CHUNKS)):
        far_copy(c).wait_send()
        near_copy(c).wait_send()
        if c >= SEP_CHUNKS:
            near_copy(c).wait_recv()
    received[...] = other[...]


def quad_factor_stage(pieces):
    half_gx, half_gy = lax.axis_size("gx") // 2, lax.axis_size("gy") // 2
    copies = pltpu.SemaphoreType.DMA((len(CHUNKS),))
    return pl.pallas_call(
        functools.partial(quad_factor_kernel, half_gx, half_gy),
        out_shape=(SQUARE, SQUARE, PIECES),
        in_specs=[VMEM],
        out_specs=(VMEM,) * 3,
        scratch_shapes=[
            pltpu.VMEM((BLOCKS, B, B), F32),
            pltpu.VMEM((NS, NB), F32),
            pltpu.VMEM((B, 2 * B), F32),
            copies,
            copies,
            copies,
            copies,
        ],
        compiler_params=pltpu.CompilerParams(collective_id=0, has_side_effects=True, vmem_limit_bytes=24 * 2**20),
        cost_estimate=pl.CostEstimate(flops=10**10, bytes_accessed=4 * 10**6, transcendentals=0),
        name="quad_factor",
    )(pieces)


def factor_stage(own, other):
    return pl.pallas_call(
        factor_kernel,
        out_shape=(jax.ShapeDtypeStruct((NS, NS), F32), jax.ShapeDtypeStruct((NS, NS), F32)),
        in_specs=[VMEM, VMEM],
        out_specs=(VMEM, VMEM),
        scratch_shapes=[pltpu.VMEM((NS, NB), F32), pltpu.VMEM((B, 2 * B), F32)],
        cost_estimate=pl.CostEstimate(flops=10**10, bytes_accessed=4 * 10**6, transcendentals=0),
        compiler_params=pltpu.CompilerParams(vmem_limit_bytes=16 * 2**20),
        name="factor",
    )(own, other)


def gather_rows(rs_own, rs_other, source, bt):
    for a in range(8):

        @pl.when(source[a] < 4)
        def _(a=a):
            bt[B * a : B * a + B, :] = rs_own[pl.ds(pl.multiple_of(B * source[a], B), B), :]

        @pl.when(source[a] >= 4)
        def _(a=a):
            bt[B * a : B * a + B, :] = rs_other[pl.ds(pl.multiple_of(B * (source[a] - 4), B), B), :]


def spread_rest(rr_own, rr_other, blocks):
    for h, rr in enumerate((rr_own, rr_other)):
        for t, (a, b) in enumerate(LOWER):
            block = rr[t]
            blocks[16 * h + 4 * a + b] = block
            if a != b:
                blocks[16 * h + 4 * b + a] = block.T
    blocks[32] = jnp.zeros((B, B), F32)


def block_at(source, a, b):
    sa, sb = source[a], source[b]
    same = (sa < 4) == (sb < 4)
    return jnp.where(same, jnp.where(sa < 4, 0, 16) + 4 * (sa % 4) + sb % 4, 32)


def pair_order(pair_ref, quad_ref):
    order = order_of([quad_ref[0, i] for i in range(8)])
    where = source_of([pair_ref[0, i] for i in range(8)])
    return order, [sum(jnp.where(order[a] == u, where[u], 0) for u in range(8)) for a in range(8)]


def pair_solve_kernel(pair_ref, quad_ref, l_ref, inverse, rs_own, rs_other, panel, ss, rs, rr, bt, vt):
    order, source = pair_order(pair_ref, quad_ref)
    gather_rows(rs_own, rs_other, source, bt)
    panel[0:NS, :] = l_ref[...]

    def store(i, rows):
        panel[pl.ds(pl.multiple_of(NS + B * order[i], B), B), :] = rows

    solve_rows(bt, inverse[...], vt, store)
    v2 = split(vt[...])
    sep_product(v2, setter(ss, lambda t, block: block))
    rest_product(v2, rs_setter(rs, lambda a, b, block: block), setter(rr, lambda t, block: block))


def pair_update_kernel(pair_ref, quad_ref, ss_in, rs_in, rr_in, rr_own, rr_other, out, blocks):
    _, source = pair_order(pair_ref, quad_ref)
    spread_rest(rr_own, rr_other, blocks)
    for t, (a, b) in enumerate(LOWER):
        out[t] = blocks[block_at(source, a, b)] - ss_in[t]
        out[RR0 + t] = blocks[block_at(source, 4 + a, 4 + b)] - rr_in[t]
    for a in range(4):
        for b in range(4):
            out[RS0 + 4 * a + b] = blocks[block_at(source, 4 + a, b)] - rs_in[B * a : B * a + B, B * b : B * b + B]


LOWER10 = jax.ShapeDtypeStruct((10, B, B), F32)
SQUARE = jax.ShapeDtypeStruct((NS, NS), F32)
PIECES = jax.ShapeDtypeStruct((BLOCKS, B, B), F32)
PANEL = jax.ShapeDtypeStruct((NJ, NS), F32)


def params(mib):
    return pltpu.CompilerParams(vmem_limit_bytes=mib * 2**20)


def pair_stage(pair, quad, l_full, inverse, rs_own, rs_other, rr_own, rr_other):
    panel, ss, rs, rr = pl.pallas_call(
        pair_solve_kernel,
        out_shape=(PANEL, LOWER10, SQUARE, LOWER10),
        in_specs=[SMEM, SMEM] + [VMEM] * 4,
        out_specs=(VMEM,) * 4,
        scratch_shapes=[pltpu.VMEM((NB, NS), F32), pltpu.VMEM((NB, NS), F32)],
        compiler_params=params(32),
        cost_estimate=pl.CostEstimate(flops=3 * 10**9, bytes_accessed=10**7, transcendentals=0),
        name="pair_solve",
    )(pair, quad, l_full, inverse, rs_own, rs_other)
    pieces = pl.pallas_call(
        pair_update_kernel,
        out_shape=PIECES,
        in_specs=[SMEM, SMEM] + [VMEM] * 5,
        out_specs=VMEM,
        scratch_shapes=[pltpu.VMEM((33, B, B), F32)],
        compiler_params=params(24),
        cost_estimate=pl.CostEstimate(flops=10**6, bytes_accessed=10**7, transcendentals=0),
        name="pair_update",
    )(pair, quad, ss, rs, rr, rr_own, rr_other)
    return panel, pieces


def quad_solve_kernel(quad_ref, l_ref, inverse, own, other, panel, lower, bt, vt):
    source = source_of([quad_ref[0, i] for i in range(8)])
    for h, pieces in enumerate((own, other)):
        for a in range(8):

            @pl.when(source[a] // 4 == h)
            def _(a=a, h=h, pieces=pieces):
                for b in range(4):
                    bt[B * a : B * a + B, B * b : B * b + B] = pieces[RS0 + 4 * (source[a] - 4 * h) + b]

    panel[0:NS, :] = l_ref[...]

    def store(i, rows):
        panel[NS + B * i : NS + B * i + B, :] = rows

    solve_rows(bt, inverse[...], vt, store)
    v2 = split(vt[...])
    for h in range(4):
        rows = slice(256 * h, 256 * (h + 1))
        last = 256 * (h + 1)
        lower[rows, 0:last] = dot3((v2[0][rows], v2[1][rows]), (v2[0][0:last], v2[1][0:last]), NT)


def quad_update_kernel(quad_ref, lower, own, other, update, blocks):
    source = source_of([quad_ref[0, i] for i in range(8)])
    spread_rest(own.at[RR0:BLOCKS], other.at[RR0:BLOCKS], blocks)
    for a in range(8):
        for b in range(a + 1):
            block = blocks[block_at(source, a, b)] - lower[B * a : B * a + B, B * b : B * b + B]
            update[B * a : B * a + B, B * b : B * b + B] = block
            if a != b:
                update[B * b : B * b + B, B * a : B * a + B] = block.T


def quad_stage(quad, l_full, inverse, own, other):
    panel, lower = pl.pallas_call(
        quad_solve_kernel,
        out_shape=(PANEL, jax.ShapeDtypeStruct((NB, NB), F32)),
        in_specs=[SMEM] + [VMEM] * 4,
        out_specs=(VMEM, VMEM),
        scratch_shapes=[pltpu.VMEM((NB, NS), F32), pltpu.VMEM((NB, NS), F32)],
        compiler_params=params(32),
        cost_estimate=pl.CostEstimate(flops=4 * 10**9, bytes_accessed=10**7, transcendentals=0),
        name="quad_solve",
    )(quad, l_full, inverse, own, other)
    update = pl.pallas_call(
        quad_update_kernel,
        out_shape=jax.ShapeDtypeStruct((NB, NB), F32),
        in_specs=[SMEM] + [VMEM] * 3,
        out_specs=VMEM,
        scratch_shapes=[pltpu.VMEM((33, B, B), F32)],
        compiler_params=params(24),
        cost_estimate=pl.CostEstimate(flops=10**6, bytes_accessed=10**7, transcendentals=0),
        name="quad_update",
    )(quad, lower, own, other)
    return panel, update


def swapped(value, axis):
    size = lax.axis_size(axis)
    return lax.ppermute(value, axis, [(i, (i + size // 2) % size) for i in range(size)])


def shards(leaf_front, place_pairs, place_quads):
    ss, rest = leaf_stage(leaf_front, place_pairs)
    other_ss = swapped(ss, "gx")
    rs, rr = rest()
    other_rs, other_rr = swapped(rs, "gx"), swapped(rr, "gx")
    l_pair, inverse = factor_stage(ss, other_ss)
    pair_panel, pieces = pair_stage(place_pairs, place_quads, l_pair, inverse, rs, other_rs, rr, other_rr)
    l_quad, inverse, other = quad_factor_stage(pieces)
    quad_panel, quad_update = quad_stage(place_quads, l_quad, inverse, pieces, other)
    return pair_panel, quad_panel, quad_update


def solution(mesh):
    spec = P("gx", "gy")
    return jax.shard_map(shards, mesh=mesh, in_specs=(spec,) * 3, out_specs=(spec,) * 3, check_vma=False)
```

```python
import functools

import jax
import jax.numpy as jnp
from jax import lax
from jax.experimental import pallas as pl
from jax.experimental.pallas import tpu as pltpu
from jax.sharding import PartitionSpec as P

F32 = jnp.float32
BF16 = jnp.bfloat16
B = 128
NS = 512
NB = 1024
NJ = 1536
LOWER = [(a, b) for a in range(4) for b in range(a + 1)]
VMEM = pl.BlockSpec(memory_space=pltpu.VMEM)
MESH = pl.DeviceIdType.MESH
RS0, RR0, BLOCKS = 10, 26, 36
CHUNKS = [(2 * i, 2) for i in range(5)] + [(RS0 + 4 * i, 4) for i in range(4)] + [(RR0, 4), (RR0 + 4, 6)]
SEP_CHUNKS = 5
FORWARD = [(5, 6, 7), (8, 9), (10,), ()]
SMEM = pl.BlockSpec(memory_space=pltpu.SMEM)
ANY = pl.BlockSpec(memory_space=pltpu.HBM)


def full(x):
    return jnp.broadcast_to(x, (8, B))


def split(x):
    hi = x.astype(BF16)
    return hi, (x - hi.astype(F32)).astype(BF16)


def dot3(a, b, dims):
    def one(x, y):
        return lax.dot_general(x, y, (dims, ((), ())), preferred_element_type=F32)

    return (one(a[1], b[0]) + one(a[0], b[1])) + one(a[0], b[0])


NN = ((1,), (0,))
NT = ((1,), (1,))


def factor_columns(m, p, last):
    r = 8 * p
    xs = [full(m[r + i : r + i + 1, 0:B]) for i in range(8)]
    ys = [full(m[r + i : r + i + 1, B : 2 * B]) for i in range(8)]
    e = [[full(xs[i][:, r + j : r + j + 1]) if j >= i else None for j in range(8)] for i in range(8)]
    inv = [None] * 8
    for k in range(8):
        inv[k] = lax.rsqrt(e[k][k])
        for j in range(k + 1, 8):
            e[k][j] = e[k][j] * inv[k]
        xs[k], ys[k] = xs[k] * inv[k], ys[k] * inv[k]
        for i in range(k + 1, 8):
            for j in range(i, 8):
                e[i][j] = e[i][j] - e[k][i] * e[k][j]
            xs[i] = xs[i] - e[k][i] * xs[k]
            ys[i] = ys[i] - e[k][i] * ys[k]
    for k in range(8):
        m[r + k : r + k + 1, 0:B] = xs[k][0:1, :]
        m[r + k : r + k + 1, B : 2 * B] = ys[k][0:1, :]
    for q in range(p + 1, last):
        t = 8 * q
        y0, y1 = m[t : t + 8, 0:B], m[t : t + 8, B : 2 * B]
        c = [full(y0[:, r + j : r + j + 1]) for j in range(8)]
        for k in range(8):
            c[k] = c[k] * inv[k]
            for j in range(k + 1, 8):
                c[j] = c[j] - c[k] * e[k][j]
            y0 = y0 - c[k] * xs[k]
            y1 = y1 - c[k] * ys[k]
        m[t : t + 8, 0:B] = y0
        m[t : t + 8, B : 2 * B] = y1


def factor_block(m):
    half = B // 2
    for p in range(half // 8):
        factor_columns(m, p, half // 8)
    top = m[0:half, :]
    below = top[:, 0:B].T
    m[half:B, :] = m[half:B, :] - dot3(split(below[half:B, :]), split(top), NN)
    for p in range(half // 8, B // 8):
        factor_columns(m, p, B // 8)


def eye_block():
    i0 = lax.broadcasted_iota(jnp.int32, (B, B), 0)
    i1 = lax.broadcasted_iota(jnp.int32, (B, B), 1)
    return i0, i1, jnp.where(i0 == i1, 1.0, 0.0).astype(F32)


def factor_front(g, m, l_ref, after=lambda step: None):
    i0, i1, eye = eye_block()
    m[:, 0:B] = g[0:B, 0:B]
    m[:, B : 2 * B] = eye
    l_ref[...] = jnp.zeros((NS, NS), F32)

    def step(k, carry):
        factor_block(m)
        for kk in range(4):

            @pl.when(k == kk)
            def _(kk=kk):
                after(kk)
                c, n = B * kk, B * (kk + 1)
                inverse = m[:, B : 2 * B]
                l_ref[c:n, c:n] = jnp.where(i0 <= i1, m[:, 0:B], 0.0).T
                g[c:n, NS + c : NS + n] = inverse
                inv2 = split(inverse)
                if kk > 0:
                    g[c:n, NS : NS + c] = dot3(inv2, split(g[c:n, NS : NS + c]), NN)
                if kk < 3:
                    right = dot3(inv2, split(g[c:n, n:NS]), NN)
                    below = right.T
                    l_ref[n:NS, c:n] = below
                    below2 = split(below)
                    g[n:NS, n:NS] = g[n:NS, n:NS] - dot3(below2, split(right), NN)
                    m[:, 0:B] = g[n : n + B, n : n + B]
                    m[:, B : 2 * B] = eye
                    g[n:NS, NS : NS + n] = g[n:NS, NS : NS + n] - dot3(below2, split(g[c:n, NS : NS + n]), NN)

        return carry

    lax.fori_loop(0, 4, step, 0)


def solve_rows(bt, g, vt, store):
    inv2 = split(g)
    for h in range(4):
        rows = dot3(split(bt[256 * h : 256 * (h + 1), :]), inv2, NT)
        vt[256 * h : 256 * (h + 1), :] = rows
        store(2 * h, rows[0:B])
        store(2 * h + 1, rows[B : 2 * B])


def order_of(place):
    rank = [sum((place[j] < place[i]).astype(jnp.int32) for j in range(8) if j != i) for i in range(8)]
    return [sum(jnp.where(rank[i] == a, i, 0) for i in range(8)) for a in range(8)]


def source_of(place):
    named, before, result = [], 0, []
    for u in range(8):
        mine = sum((place[i] == 4 + u).astype(jnp.int32) for i in range(8))
        result.append(jnp.where(mine == 1, before, 4 + u - before))
        before = before + mine
    return result


def leaf_solve_kernel(place_ref, leaf, vt, ss, g, m, bt, base, l_buf, sems):
    order = order_of([place_ref[0, i] for i in range(8)])
    at = [pl.multiple_of(NS + B * order[a], B) for a in range(8)]
    first = pltpu.make_async_copy(leaf.at[0:NS, 0:NS], g.at[:, 0:NS], sems.at[0])
    first.start()
    copies = [pltpu.make_async_copy(leaf.at[pl.ds(at[a], B), 0:NS], bt.at[B * a : B * a + B], sems.at[1 + a]) for a in range(8)]
    copies += [
        pltpu.make_async_copy(leaf.at[pl.ds(at[a], B), pl.ds(at[b], B)], base.at[t], sems.at[9 + t])
        for t, (a, b) in enumerate(LOWER)
    ]
    for copy in copies:
        copy.start()
    g[:, NS:NB] = jnp.zeros((NS, NS), F32)
    first.wait()
    factor_front(g, m, l_buf)
    for copy in copies:
        copy.wait()
    solve_rows(bt, g[:, NS:NB], vt, lambda i, rows: None)
    sep_product(split(vt[0:NS, :]), setter(ss, lambda t, block: base[t] - block))


def sep_product(v2, put):
    for h in range(2):
        rows = slice(256 * h, 256 * (h + 1))
        prod = dot3((v2[0][rows], v2[1][rows]), (v2[0][0 : 256 * (h + 1)], v2[1][0 : 256 * (h + 1)]), NT)
        for t, (a, b) in enumerate(LOWER):
            if a // 2 == h:
                put(t, prod[B * (a % 2) : B * (a % 2) + B, B * b : B * b + B])


def rest_product(v2, put_rs, put_rr):
    for h in range(2):
        rows = slice(NS + 256 * h, NS + 256 * (h + 1))
        last = NS + 256 * (h + 1)
        prod = dot3((v2[0][rows], v2[1][rows]), (v2[0][0:last], v2[1][0:last]), NT)
        for a in (2 * h, 2 * h + 1):
            r = B * (a % 2)
            for b in range(4):
                put_rs(a, b, prod[r : r + B, B * b : B * b + B])
        for t, (a, b) in enumerate(LOWER):
            if a // 2 == h:
                put_rr(t, prod[B * (a % 2) : B * (a % 2) + B, NS + B * b : NS + B * b + B])


def setter(ref, value):
    def put(t, block):
        ref[t] = value(t, block)

    return put


def rs_setter(ref, value):
    def put(a, b, block):
        ref[B * a : B * a + B, B * b : B * b + B] = value(a, b, block)

    return put


def leaf_rest_kernel(place_ref, leaf, vt, rs, rr, rs_buf, rr_buf, sems):
    order = order_of([place_ref[0, i] for i in range(8)])
    at = [pl.multiple_of(NS + B * order[a], B) for a in range(8)]
    copies = [
        pltpu.make_async_copy(leaf.at[pl.ds(at[4 + a], B), pl.ds(at[b], B)], rs_buf.at[4 * a + b], sems.at[4 * a + b])
        for a in range(4)
        for b in range(4)
    ]
    copies += [
        pltpu.make_async_copy(leaf.at[pl.ds(at[4 + a], B), pl.ds(at[4 + b], B)], rr_buf.at[t], sems.at[16 + t])
        for t, (a, b) in enumerate(LOWER)
    ]
    for copy in copies:
        copy.start()
    for copy in copies:
        copy.wait()
    rest_product(
        split(vt[...]),
        rs_setter(rs, lambda a, b, block: rs_buf[4 * a + b] - block),
        setter(rr, lambda t, block: rr_buf[t] - block),
    )


def leaf_stage(leaf, place):
    vt, ss = pl.pallas_call(
        leaf_solve_kernel,
        out_shape=(jax.ShapeDtypeStruct((NB, NS), F32), jax.ShapeDtypeStruct((10, B, B), F32)),
        in_specs=[SMEM, ANY],
        out_specs=(VMEM, VMEM),
        scratch_shapes=[
            pltpu.VMEM((NS, NB), F32),
            pltpu.VMEM((B, 2 * B), F32),
            pltpu.VMEM((NB, NS), F32),
            pltpu.VMEM((10, B, B), F32),
            pltpu.VMEM((NS, NS), F32),
            pltpu.SemaphoreType.DMA((19,)),
        ],
        cost_estimate=pl.CostEstimate(flops=10**10, bytes_accessed=10**7, transcendentals=0),
        compiler_params=pltpu.CompilerParams(vmem_limit_bytes=54 * 2**20),
        name="leaf_solve",
    )(place, leaf)

    def rest():
        return pl.pallas_call(
            leaf_rest_kernel,
            out_shape=(jax.ShapeDtypeStruct((NS, NS), F32), jax.ShapeDtypeStruct((10, B, B), F32)),
            in_specs=[SMEM, ANY, VMEM],
            out_specs=(VMEM, VMEM),
            scratch_shapes=[pltpu.VMEM((16, B, B), F32), pltpu.VMEM((10, B, B), F32), pltpu.SemaphoreType.DMA((26,))],
            cost_estimate=pl.CostEstimate(flops=3 * 10**9, bytes_accessed=10**7, transcendentals=0),
            compiler_params=pltpu.CompilerParams(vmem_limit_bytes=54 * 2**20),
            name="leaf_rest",
        )(place, leaf, vt)

    return ss, rest


def factor_kernel(own, other, l_ref, inverse, g, m):
    joined_separator(own, other, g)
    factor_front(g, m, l_ref)
    inverse[...] = g[:, NS:NB]


def joined_separator(own, other, g):
    for t, (a, b) in enumerate(LOWER):
        block = own[t] + other[t]
        g[B * a : B * a + B, B * b : B * b + B] = block
        if a != b:
            g[B * b : B * b + B, B * a : B * a + B] = block.T
    g[:, NS:NB] = jnp.zeros((NS, NS), F32)


def quad_factor_kernel(half_gx, half_gy, own, l_ref, inverse, received, other, g, m, far_send, far_recv, near_send, near_recv):
    gx, gy = lax.axis_index("gx"), lax.axis_index("gy")
    side = gx // half_gx
    far = (gx, lax.rem(gy + half_gy, 2 * half_gy))
    near = (lax.rem(gx + half_gx, 2 * half_gx), gy)
    barrier = pltpu.get_barrier_semaphore()
    for device in (far, near):
        pl.semaphore_signal(barrier, inc=1, device_id=device, device_id_type=MESH)
    pl.semaphore_wait(barrier, 2)

    def far_copy(c):
        start, count = CHUNKS[c]
        part = pl.ds(start + side * (count // 2), count // 2)
        return pltpu.make_async_remote_copy(
            own.at[part], other.at[part], far_send.at[c], far_recv.at[c], device_id=far, device_id_type=MESH
        )

    def near_copy(c):
        start, count = CHUNKS[c]
        part = pl.ds(start + side * (count // 2), count // 2)
        return pltpu.make_async_remote_copy(
            other.at[part], other.at[part], near_send.at[c], near_recv.at[c], device_id=near, device_id_type=MESH
        )

    def forward(c):
        far_copy(c).wait_recv()
        near_copy(c).start()

    for c in range(len(CHUNKS)):
        far_copy(c).start()
    for c in range(SEP_CHUNKS):
        forward(c)
    for c in range(SEP_CHUNKS):
        near_copy(c).wait_recv()
    joined_separator(own, other, g)

    def after(step):
        for c in FORWARD[step]:
            forward(c)

    factor_front(g, m, l_ref, after)
    inverse[...] = g[:, NS:NB]
    for c in range(len(CHUNKS)):
        far_copy(c).wait_send()
        near_copy(c).wait_send()
        if c >= SEP_CHUNKS:
            near_copy(c).wait_recv()
    received[...] = other[...]


def quad_factor_stage(pieces):
    half_gx, half_gy = lax.axis_size("gx") // 2, lax.axis_size("gy") // 2
    copies = pltpu.SemaphoreType.DMA((len(CHUNKS),))
    return pl.pallas_call(
        functools.partial(quad_factor_kernel, half_gx, half_gy),
        out_shape=(SQUARE, SQUARE, PIECES),
        in_specs=[VMEM],
        out_specs=(VMEM,) * 3,
        scratch_shapes=[
            pltpu.VMEM((BLOCKS, B, B), F32),
            pltpu.VMEM((NS, NB), F32),
            pltpu.VMEM((B, 2 * B), F32),
            copies,
            copies,
            copies,
            copies,
        ],
        compiler_params=pltpu.CompilerParams(collective_id=0, has_side_effects=True, vmem_limit_bytes=24 * 2**20),
        cost_estimate=pl.CostEstimate(flops=10**10, bytes_accessed=4 * 10**6, transcendentals=0),
        name="quad_factor",
    )(pieces)


def factor_stage(own, other):
    return pl.pallas_call(
        factor_kernel,
        out_shape=(jax.ShapeDtypeStruct((NS, NS), F32), jax.ShapeDtypeStruct((NS, NS), F32)),
        in_specs=[VMEM, VMEM],
        out_specs=(VMEM, VMEM),
        scratch_shapes=[pltpu.VMEM((NS, NB), F32), pltpu.VMEM((B, 2 * B), F32)],
        cost_estimate=pl.CostEstimate(flops=10**10, bytes_accessed=4 * 10**6, transcendentals=0),
        compiler_params=pltpu.CompilerParams(vmem_limit_bytes=16 * 2**20),
        name="factor",
    )(own, other)


def gather_rows(rs_own, rs_other, source, bt):
    for a in range(8):

        @pl.when(source[a] < 4)
        def _(a=a):
            bt[B * a : B * a + B, :] = rs_own[pl.ds(pl.multiple_of(B * source[a], B), B), :]

        @pl.when(source[a] >= 4)
        def _(a=a):
            bt[B * a : B * a + B, :] = rs_other[pl.ds(pl.multiple_of(B * (source[a] - 4), B), B), :]


def spread_rest(rr_own, rr_other, blocks):
    for h, rr in enumerate((rr_own, rr_other)):
        for t, (a, b) in enumerate(LOWER):
            block = rr[t]
            blocks[16 * h + 4 * a + b] = block
            if a != b:
                blocks[16 * h + 4 * b + a] = block.T
    blocks[32] = jnp.zeros((B, B), F32)


def block_at(source, a, b):
    sa, sb = source[a], source[b]
    same = (sa < 4) == (sb < 4)
    return jnp.where(same, jnp.where(sa < 4, 0, 16) + 4 * (sa % 4) + sb % 4, 32)


def pair_order(pair_ref, quad_ref):
    order = order_of([quad_ref[0, i] for i in range(8)])
    where = source_of([pair_ref[0, i] for i in range(8)])
    return order, [sum(jnp.where(order[a] == u, where[u], 0) for u in range(8)) for a in range(8)]


def pair_solve_kernel(pair_ref, quad_ref, l_ref, inverse, rs_own, rs_other, panel, ss, rs, rr, bt, vt):
    order, source = pair_order(pair_ref, quad_ref)
    gather_rows(rs_own, rs_other, source, bt)
    panel[0:NS, :] = l_ref[...]

    def store(i, rows):
        panel[pl.ds(pl.multiple_of(NS + B * order[i], B), B), :] = rows

    solve_rows(bt, inverse[...], vt, store)
    v2 = split(vt[...])
    sep_product(v2, setter(ss, lambda t, block: block))
    rest_product(v2, rs_setter(rs, lambda a, b, block: block), setter(rr, lambda t, block: block))


def pair_update_kernel(pair_ref, quad_ref, ss_in, rs_in, rr_in, rr_own, rr_other, out, blocks):
    _, source = pair_order(pair_ref, quad_ref)
    spread_rest(rr_own, rr_other, blocks)
    for t, (a, b) in enumerate(LOWER):
        out[t] = blocks[block_at(source, a, b)] - ss_in[t]
        out[RR0 + t] = blocks[block_at(source, 4 + a, 4 + b)] - rr_in[t]
    for a in range(4):
        for b in range(4):
            out[RS0 + 4 * a + b] = blocks[block_at(source, 4 + a, b)] - rs_in[B * a : B * a + B, B * b : B * b + B]


LOWER10 = jax.ShapeDtypeStruct((10, B, B), F32)
SQUARE = jax.ShapeDtypeStruct((NS, NS), F32)
PIECES = jax.ShapeDtypeStruct((BLOCKS, B, B), F32)
PANEL = jax.ShapeDtypeStruct((NJ, NS), F32)


def params(mib):
    return pltpu.CompilerParams(vmem_limit_bytes=mib * 2**20)


def pair_stage(pair, quad, l_full, inverse, rs_own, rs_other, rr_own, rr_other):
    panel, ss, rs, rr = pl.pallas_call(
        pair_solve_kernel,
        out_shape=(PANEL, LOWER10, SQUARE, LOWER10),
        in_specs=[SMEM, SMEM] + [VMEM] * 4,
        out_specs=(VMEM,) * 4,
        scratch_shapes=[pltpu.VMEM((NB, NS), F32), pltpu.VMEM((NB, NS), F32)],
        compiler_params=params(32),
        cost_estimate=pl.CostEstimate(flops=3 * 10**9, bytes_accessed=10**7, transcendentals=0),
        name="pair_solve",
    )(pair, quad, l_full, inverse, rs_own, rs_other)
    pieces = pl.pallas_call(
        pair_update_kernel,
        out_shape=PIECES,
        in_specs=[SMEM, SMEM] + [VMEM] * 5,
        out_specs=VMEM,
        scratch_shapes=[pltpu.VMEM((33, B, B), F32)],
        compiler_params=params(24),
        cost_estimate=pl.CostEstimate(flops=10**6, bytes_accessed=10**7, transcendentals=0),
        name="pair_update",
    )(pair, quad, ss, rs, rr, rr_own, rr_other)
    return panel, pieces


def quad_kernel(quad_ref, l_ref, inverse, own, other, panel, update, bt, vt, blocks):
    source = source_of([quad_ref[0, i] for i in range(8)])
    for h, pieces in enumerate((own, other)):
        for a in range(8):

            @pl.when(source[a] // 4 == h)
            def _(a=a, h=h, pieces=pieces):
                for b in range(4):
                    bt[B * a : B * a + B, B * b : B * b + B] = pieces[RS0 + 4 * (source[a] - 4 * h) + b]

    panel[0:NS, :] = l_ref[...]

    def store(i, rows):
        panel[NS + B * i : NS + B * i + B, :] = rows

    solve_rows(bt, inverse[...], vt, store)
    spread_rest(own.at[RR0:BLOCKS], other.at[RR0:BLOCKS], blocks)
    v2 = split(vt[...])
    for h in range(4):
        rows = slice(256 * h, 256 * (h + 1))
        last = 256 * (h + 1)
        prod = dot3((v2[0][rows], v2[1][rows]), (v2[0][0:last], v2[1][0:last]), NT)
        for a in (2 * h, 2 * h + 1):
            r = B * (a % 2)
            for b in range(a + 1):
                block = blocks[block_at(source, a, b)] - prod[r : r + B, B * b : B * b + B]
                update[B * a : B * a + B, B * b : B * b + B] = block
                if a != b:
                    update[B * b : B * b + B, B * a : B * a + B] = block.T


def quad_stage(quad, l_full, inverse, own, other):
    return pl.pallas_call(
        quad_kernel,
        out_shape=(PANEL, jax.ShapeDtypeStruct((NB, NB), F32)),
        in_specs=[SMEM] + [VMEM] * 4,
        out_specs=(VMEM, VMEM),
        scratch_shapes=[pltpu.VMEM((NB, NS), F32), pltpu.VMEM((NB, NS), F32), pltpu.VMEM((33, B, B), F32)],
        compiler_params=params(32),
        cost_estimate=pl.CostEstimate(flops=4 * 10**9, bytes_accessed=10**7, transcendentals=0),
        name="quad",
    )(quad, l_full, inverse, own, other)


def swapped(value, axis):
    size = lax.axis_size(axis)
    return lax.ppermute(value, axis, [(i, (i + size // 2) % size) for i in range(size)])


def shards(leaf_front, place_pairs, place_quads):
    ss, rest = leaf_stage(leaf_front, place_pairs)
    other_ss = swapped(ss, "gx")
    rs, rr = rest()
    other_rs, other_rr = swapped(rs, "gx"), swapped(rr, "gx")
    l_pair, inverse = factor_stage(ss, other_ss)
    pair_panel, pieces = pair_stage(place_pairs, place_quads, l_pair, inverse, rs, other_rs, rr, other_rr)
    l_quad, inverse, other = quad_factor_stage(pieces)
    quad_panel, quad_update = quad_stage(place_quads, l_quad, inverse, pieces, other)
    return pair_panel, quad_panel, quad_update


def solution(mesh):
    spec = P("gx", "gy")
    return jax.shard_map(shards, mesh=mesh, in_specs=(spec,) * 3, out_specs=(spec,) * 3, check_vma=False)
```
